256 devices in a mesh: seq: 64 (over y, z, core), tp: 4 (over x).
Axes of the slice: x: 4, y: 4, z: 8, core: 2. Of those that a mesh axis runs over, the one named last changes fastest.
Arguments:
- inputs: bfloat16 [4, 4, 1024], P(None, None, 'tp'), may hold values from -64 to 64
- attention_gain: bfloat16 [1024], replicated, may hold values from 0.099609375 to 1.8984375
- forward_gain: bfloat16 [1024], replicated, may hold values from 0.099609375 to 1.8984375
- query_weight: bfloat16 [1024, 1024], P(None, 'tp'), may hold values from -0.1875 to 0.1875
- key_weight: bfloat16 [1024, 1024], P(None, 'tp'), may hold values from -0.1875 to 0.1875
- value_weight: bfloat16 [1024, 1024], P(None, 'tp'), may hold values from -0.1875 to 0.1875
- output_weight: bfloat16 [1024, 1024], P('tp'), may hold values from -0.1875 to 0.1875
- gate_weight: bfloat16 [1024, 4096], P(None, 'tp'), may hold values from -0.1875 to 0.1875
- up_weight: bfloat16 [1024, 4096], P(None, 'tp'), may hold values from -0.1875 to 0.1875
- down_weight: bfloat16 [4096, 1024], P('tp'), may hold values from -0.09375 to 0.09375
- variate_bias: float32 [2, 16], replicated, may hold values from -256 to 256
- cache_keys: bfloat16 [4, 32768, 1024], P(None, 'seq', 'tp'), may hold values from -15 to 15
- cache_values: bfloat16 [4, 32768, 1024], P(None, 'seq', 'tp'), may hold values from -12 to 12
- cache_variates: int32 [4, 32768], P(None, 'seq'), may hold values from 0 to 7
- cache_mask: int32 [4, 32768], P(None, 'seq'), may hold values 0 or 1
- cache_lengths: int32 [4], replicated, may hold values from 1 to 32768, as said below
- fresh_flags: int32 [4], replicated, may hold values 0 or 1
- new_variates: int32 [4, 4], replicated, may hold values from 0 to 7
- new_times: int32 [4, 4], replicated, may hold values from 0 to 32771
Outputs:
- hidden_states: bfloat16 [4, 4, 1024], P(None, None, 'tp')
- new_keys: bfloat16 [4, 4, 1024], P(None, None, 'tp')
- new_values: bfloat16 [4, 4, 1024], P(None, None, 'tp')
The draws below stay inside these ranges and needn't reach their ends.
Inputs may be any that keep to these rules, and one draw needn't show every extreme that they name: `cache_lengths`: some request has exactly 32768 filled positions.
All inputs are finite; a program needn't handle non-finite values. No bound on the sum of `cache_mask` on one device may be relied on, other than what follows from the above.
Results may differ from the reference program's by a relative error of at most 0.014.
Values may be sent and summed in bfloat16 or wider, within the bound.
A program may use at most 64 MiB of HBM per device.

```python
import math
import jax
import jax.numpy as jnp
from jax import lax

D = 1024
HEADS = 16
HEAD_DIM = 64
FF = 4096
REQ = 4
STEPS = 4
VARIATES = 8
CACHE = 32768


def draw_inputs(key, part):
    key_cols, key_rows, key_base = jax.random.split(key, 3)
    ramp = jnp.exp(jnp.linspace(-0.55, 0.55, D, dtype=jnp.float32))
    columns = ramp * jnp.exp(jax.random.uniform(key_cols, (D,), jnp.float32, -0.6, 0.6))
    row_scale = jnp.exp(jax.random.uniform(key_rows, (REQ, STEPS, 1), jnp.float32, -1.15, 1.15))
    base = jnp.clip(jax.random.normal(key_base, (REQ, STEPS, D), jnp.float32), -5.0, 5.0)
    return (base * columns[None, None, :] * row_scale).astype(jnp.bfloat16)


def draw_variate_bias(key, part):
    key_base = jax.random.fold_in(key, 0)
    base = jnp.clip(jax.random.normal(key_base, (2, HEADS), jnp.float32), -6.0, 6.0) * 1.5
    return base


def draw_cache_lengths(key, part):
    key_len, key_top = jax.random.split(key, 2)
    lengths = jax.random.randint(key_len, (REQ,), 1, CACHE + 1)
    chosen = jax.random.randint(key_top, (), 0, REQ)
    return jnp.where(jnp.arange(REQ) == chosen, CACHE, lengths).astype(jnp.int32)


def with_ends(entries, key, smallest, largest):
    extent = entries.shape
    spot = [jax.random.randint(jax.random.fold_in(key, axis), (), 0, extent[axis]) for axis in range(len(extent))]
    entries = entries.at[tuple(spot)].set(smallest)
    longest = extent.index(max(extent))
    spot[longest] = (spot[longest] + 1) % extent[longest]
    return entries.at[tuple(spot)].set(largest)


def block_levels(key, extent, cuts, least, top_value):
    def one(dim, blocks):
        steps = jax.random.uniform(jax.random.fold_in(jax.random.fold_in(key, 6), dim), (blocks,), jnp.float32, least / len(cuts), top_value / len(cuts))
        return jnp.repeat(jnp.exp(steps), extent[dim] // blocks).reshape((-1,) + (1,) * (len(extent) - dim - 1))

    level = one(*cuts[0])
    for cut in cuts[1:]:
        level = level * one(*cut)
    return level


def gaussian(key, shape, deviation, reach, shards=(), kind=jnp.bfloat16):
    factor_of = block_levels(key, shape, shards, -0.22, 0.18) if shards else 1.0
    entries = jax.random.normal(key, shape, jnp.float32) * deviation * factor_of
    return jnp.minimum(jnp.maximum(entries, -reach), reach).astype(kind)


def setup_inputs(seed: int = 0) -> dict:
    streams_of = jax.random.split(jax.random.key(seed), 20)
    return {
        "inputs": draw_inputs(jax.random.fold_in(streams_of[19], 71), 0),
        "attention_gain": jnp.clip(1.0 + 0.18 * jax.random.normal(streams_of[1], (D,), jnp.float32), 0.099609375, 1.8984375).astype(jnp.bfloat16),
        "forward_gain": jnp.clip(1.0 + 0.18 * jax.random.normal(streams_of[2], (D,), jnp.float32), 0.099609375, 1.8984375).astype(jnp.bfloat16),
        "query_weight": gaussian(streams_of[3], (D, D), D ** -0.5, 0.1875, ((1, 4),)),
        "key_weight": gaussian(streams_of[4], (D, D), D ** -0.5, 0.1875, ((1, 4),)),
        "value_weight": gaussian(streams_of[5], (D, D), D ** -0.5, 0.1875, ((1, 4),)),
        "output_weight": gaussian(streams_of[6], (D, D), D ** -0.5, 0.1875, ((0, 4),)),
        "gate_weight": gaussian(streams_of[7], (D, FF), D ** -0.5, 0.1875, ((1, 4),)),
        "up_weight": gaussian(streams_of[8], (D, FF), D ** -0.5, 0.1875, ((1, 4),)),
        "down_weight": gaussian(streams_of[9], (FF, D), FF ** -0.5, 0.09375, ((0, 4),)),
        "variate_bias": draw_variate_bias(jax.random.fold_in(streams_of[19], 71), 0),
        "cache_keys": gaussian(streams_of[11], (REQ, CACHE, D), 3.0, 15.0, ((1, 64), (2, 4))),
        "cache_values": gaussian(streams_of[12], (REQ, CACHE, D), 2.0, 12.0, ((1, 64), (2, 4))),
        "cache_variates": with_ends(jax.random.randint(streams_of[13], (REQ, CACHE), 0, VARIATES), jax.random.fold_in(streams_of[13], 1), 0, VARIATES - 1).astype(jnp.int32),
        "cache_mask": with_ends((jax.random.randint(streams_of[14], (REQ, CACHE), 0, 8) < 7).astype(jnp.int32), jax.random.fold_in(streams_of[14], 1), 0, 1),
        "cache_lengths": draw_cache_lengths(jax.random.fold_in(streams_of[19], 71), 0),
        "fresh_flags": with_ends((jax.random.randint(streams_of[16], (REQ,), 0, 8) < 1).astype(jnp.int32), jax.random.fold_in(streams_of[16], 1), 0, 1),
        "new_variates": with_ends(jax.random.randint(streams_of[17], (REQ, STEPS), 0, VARIATES), jax.random.fold_in(streams_of[17], 1), 0, VARIATES - 1).astype(jnp.int32),
        "new_times": with_ends(jax.random.randint(streams_of[18], (REQ, STEPS), 0, CACHE + STEPS), jax.random.fold_in(streams_of[18], 1), 0, (CACHE + STEPS) - 1).astype(jnp.int32),
    }


epsilon = 1e-05

def rms_apply(values, gain):
    data = values.astype(jnp.float32)
    inverse_rms = lax.rsqrt(lax.optimization_barrier(jnp.mean(data * data, axis=-1, keepdims=True)) + epsilon)
    return (data * inverse_rms * gain.astype(jnp.float32)[None, :]).astype(jnp.bfloat16)

def rotated(blocks, times):
    half = blocks.shape[-1] // 2
    ladder = jnp.arange(half, dtype=jnp.float32) * (2.0 / blocks.shape[-1])
    inverse = jnp.exp(-math.log(10000.0) * ladder)
    angles = times.astype(jnp.float32)[:, None] * inverse[None, :]
    cosine = jnp.cos(angles)[:, None, :]
    sine = jnp.sin(angles)[:, None, :]
    first = blocks[..., :half]
    second = blocks[..., half:]
    return jnp.concatenate([first * cosine - second * sine, second * cosine + first * sine], axis=-1)

def reference(inputs, attention_gain, forward_gain, query_weight, key_weight, value_weight, output_weight, gate_weight, up_weight, down_weight, variate_bias, cache_keys, cache_values, cache_variates, cache_mask, cache_lengths, fresh_flags, new_variates, new_times):
    scale = 1.0 / math.sqrt(HEAD_DIM)
    positions = jnp.arange(CACHE, dtype=jnp.int32)
    usable = (positions[None, :] < cache_lengths[:, None]) & (cache_mask == 1) & (fresh_flags[:, None] == 0)
    key_blocks = cache_keys.reshape(REQ, CACHE, HEADS, HEAD_DIM)
    value_blocks = cache_values.reshape(REQ, CACHE, HEADS, HEAD_DIM)
    same_bias = variate_bias[0].astype(jnp.float32)
    other_bias = variate_bias[1].astype(jnp.float32)
    hidden_list = []
    key_list = []
    value_list = []
    for step_index in range(STEPS):
        current = inputs[:, step_index, :]
        normed = rms_apply(current, attention_gain)
        times_now = new_times[:, step_index]
        query_full = jnp.dot(normed, query_weight, preferred_element_type=jnp.float32)
        key_full = jnp.dot(normed, key_weight, preferred_element_type=jnp.float32)
        value_full = jnp.dot(normed, value_weight, preferred_element_type=jnp.float32)
        queries_now = rotated(query_full.reshape(REQ, HEADS, HEAD_DIM), times_now).astype(jnp.bfloat16)
        keys_now = rotated(key_full.reshape(REQ, HEADS, HEAD_DIM), times_now).astype(jnp.bfloat16)
        values_now = value_full.reshape(REQ, HEADS, HEAD_DIM).astype(jnp.bfloat16)
        key_list.append(keys_now)
        value_list.append(values_now)
        fresh_keys = jnp.stack(key_list, axis=1)
        fresh_values = jnp.stack(value_list, axis=1)
        variate_now = new_variates[:, step_index]
        same_new = new_variates[:, :step_index + 1] == variate_now[:, None]

        def per_request(item):
            query_one, keys_one, values_one, usable_one, variates_one, variate_one, new_keys_one, new_values_one, same_one = item
            scores = jnp.einsum('he,che->hc', query_one.astype(jnp.float32), keys_one.astype(jnp.float32)) * scale
            scores = scores + jnp.where((variates_one == variate_one)[None, :], same_bias[:, None], other_bias[:, None])
            scores = jnp.where(usable_one[None, :], scores, -1e+30)
            new_scores = jnp.einsum('he,she->hs', query_one.astype(jnp.float32), new_keys_one.astype(jnp.float32)) * scale
            new_scores = new_scores + jnp.where(same_one[None, :], same_bias[:, None], other_bias[:, None])
            peak = jnp.maximum(lax.optimization_barrier(jnp.max(scores, axis=1)), lax.optimization_barrier(jnp.max(new_scores, axis=1)))
            raw = jnp.where(usable_one[None, :], jnp.exp(scores - peak[:, None]), 0.0)
            new_raw = jnp.exp(new_scores - peak[:, None])
            totals = lax.optimization_barrier(jnp.sum(raw, axis=1)) + lax.optimization_barrier(jnp.sum(new_raw, axis=1))
            raw_low = lax.optimization_barrier(raw.astype(jnp.bfloat16)).astype(jnp.float32)
            new_low = lax.optimization_barrier(new_raw.astype(jnp.bfloat16)).astype(jnp.float32)
            sums = jnp.einsum('hc,che->he', raw_low, values_one.astype(jnp.float32))
            sums = sums + jnp.einsum('hs,she->he', new_low, new_values_one.astype(jnp.float32))
            return (sums / totals[:, None]).reshape(HEADS * HEAD_DIM)
        attention = lax.map(per_request, (queries_now, key_blocks, value_blocks, usable, cache_variates, variate_now, fresh_keys, fresh_values, same_new)).astype(jnp.bfloat16)
        middle = (current.astype(jnp.float32) + jnp.dot(attention, output_weight, preferred_element_type=jnp.float32)).astype(jnp.bfloat16)
        normed_two = rms_apply(middle, forward_gain)
        gate_full = jnp.dot(normed_two, gate_weight, preferred_element_type=jnp.float32)
        up_full = jnp.dot(normed_two, up_weight, preferred_element_type=jnp.float32)
        activated = (jax.nn.silu(gate_full) * up_full).astype(jnp.bfloat16)
        output = (middle.astype(jnp.float32) + jnp.dot(activated, down_weight, preferred_element_type=jnp.float32)).astype(jnp.bfloat16)
        hidden_list.append(output)
    hidden_states = jnp.stack(hidden_list, axis=1)
    new_keys = jnp.stack(key_list, axis=1).reshape(REQ, STEPS, D)
    new_values = jnp.stack(value_list, axis=1).reshape(REQ, STEPS, D)
    return (hidden_states, new_keys, new_values)
```

```python
import math

import numpy as np

import jax
import jax.numpy as jnp
from jax import lax
from jax.experimental import pallas as pl
from jax.experimental.pallas import tpu as pltpu
from jax.sharding import PartitionSpec as P

D = 1024
HEAD_DIM = 64
STEPS = 4
REQ = 4
TOK = REQ * STEPS
TP = 4
LW = 256
LH = 4
SPAN = 512
NB = 8
NZ = 8
EPS = 1e-05
SCALE = 1.0 / math.sqrt(HEAD_DIM)
NEG = -1e30

MESH = pl.DeviceIdType.MESH
F32 = jnp.float32
BF16 = jnp.bfloat16


def iota(shape, axis):
    return lax.broadcasted_iota(jnp.int32, shape, axis)


def dot(a, b):
    return jnp.dot(a, b, preferred_element_type=F32)


def dot_t(a, b):
    return lax.dot_general(a, b, (((1,), (1,)), ((), ())), preferred_element_type=F32)


def merge(parts):
    peaks = [part[:, 96:97] for part in parts]
    peak = peaks[0]
    for other in peaks[1:]:
        peak = jnp.maximum(peak, other)
    joined = jnp.exp(peaks[0] - peak) * parts[0]
    for part, own in zip(parts[1:], peaks[1:]):
        joined = joined + jnp.exp(own - peak) * part
    return joined, peak


def kernel(
    x_hbm, again_hbm, fgain_hbm, wq_hbm, wk_hbm, wv_hbm, wo_hbm, wg_hbm, wu_hbm, wd_hbm,
    bias_hbm, ck_hbm, cv_hbm, cvar_hbm, cmask_hbm, clen_hbm, fresh_hbm, nvar_hbm, ntime_hbm,
    inv_hbm,
    hid_out, nk_out, nv_out,
    xg, again, fgain, wq, wk, wv, wo, wg, wu, wd,
    bias, ck, cv, cvar, cmask, clen, fresh, nvar, ntime, inv,
    xf, xb, sbuf, rslots, nbuf, zslots, cslots, midall, midf, midc, dbuf, dslots,
    hid_v, nk_v, nv_v,
    lsem, osem, ssem, rsem,
):
    s = lax.axis_index("seq")
    i = lax.axis_index("tp")
    y = s // 16
    z = lax.rem(s // 2, NZ)
    c = lax.rem(s, 2)
    b = y * 2 + c

    def tp_peer(d):
        return (s, lax.rem(i + d, TP))

    def b_peer(d):
        other = lax.rem(b + d, NB)
        return other, ((other // 2) * 16 + z * 2 + lax.rem(other, 2), i)

    def z_peer(d):
        return (y * 16 + lax.rem(z + d, NZ) * 2 + c, i)

    barrier = pltpu.get_barrier_semaphore()
    for d in range(1, TP):
        pl.semaphore_signal(barrier, inc=1, device_id=tp_peer(d), device_id_type=MESH)
    for d in range(1, NB):
        pl.semaphore_signal(barrier, inc=1, device_id=b_peer(d)[1], device_id_type=MESH)
    for d in range(1, NZ):
        pl.semaphore_signal(barrier, inc=1, device_id=z_peer(d), device_id_type=MESH)

    count = [0]

    def fetch(src, dst):
        copy = pltpu.make_async_copy(src, dst, lsem.at[count[0]])
        count[0] += 1
        copy.start()
        return copy

    x_copy = fetch(x_hbm, xg.at[i])
    time_copy = fetch(ntime_hbm, ntime)
    inv_copy = fetch(inv_hbm, inv)
    small = [
        fetch(nvar_hbm, nvar), fetch(bias_hbm, bias), fetch(clen_hbm, clen),
        fetch(fresh_hbm, fresh), fetch(cvar_hbm, cvar), fetch(cmask_hbm, cmask),
        fetch(again_hbm, again), fetch(fgain_hbm, fgain),
    ]
    qkv_copies = [fetch(wq_hbm, wq), fetch(wk_hbm, wk), fetch(wv_hbm, wv)]
    k_copies = [fetch(ck_hbm.at[r], ck.at[r]) for r in range(REQ)]
    v_copies = [fetch(cv_hbm.at[r], cv.at[r]) for r in range(REQ)]
    wo_copy = fetch(wo_hbm, wo)
    wg_copy = fetch(wg_hbm, wg)
    wu_copy = fetch(wu_hbm, wu)
    wd_copy = fetch(wd_hbm, wd)

    sends = []

    def send(src, dst, phase, peer):
        copy = pltpu.make_async_remote_copy(
            src_ref=src, dst_ref=dst, send_sem=ssem.at[len(sends)], recv_sem=rsem.at[phase],
            device_id=peer, device_id_type=MESH,
        )
        copy.start()
        sends.append(copy)

    def arrived(region, phase):
        pltpu.make_async_copy(region, region, rsem.at[phase]).wait()

    x_copy.wait()
    pl.semaphore_wait(barrier, TP - 1 + NB - 1 + NZ - 1)
    for d in range(1, TP):
        send(xg.at[i], xg.at[i], 0, tp_peer(d))

    time_copy.wait()
    inv_copy.wait()
    for copy in small:
        copy.wait()
    lane = iota((TOK, 128), 1)
    row16 = iota((TOK, 128), 0)
    times = jnp.zeros((TOK, 128), F32)
    for n in range(TOK):
        times = jnp.where(row16 == n, ntime[n // STEPS, n % STEPS].astype(F32), times)
    angles = times * inv[...]
    cosine = jnp.cos(angles)
    sine = jnp.sin(angles)
    sine = jnp.where((lane & 32) == 0, -sine, sine)
    cosine = jnp.concatenate([cosine, cosine], axis=1)
    sine = jnp.concatenate([sine, sine], axis=1)

    rowh = iota((16, 1), 0)
    same_col = jnp.zeros((16, 1), F32)
    other_col = jnp.zeros((16, 1), F32)
    for h in range(LH):
        same_col = jnp.where((rowh & 3) == h, bias[0, i * LH + h], same_col)
        other_col = jnp.where((rowh & 3) == h, bias[1, i * LH + h], other_col)
    position = s * SPAN + iota((1, SPAN), 1)
    usable = []
    biases = []
    for r in range(REQ):
        ok = (
            (position < clen[r])
            & (cmask[r:r + 1, :] == 1)
            & ((iota((1, SPAN), 1) * 0 + fresh[r]) == 0)
        )
        usable.append(jnp.where(ok, 1, 0))
        var_col = jnp.zeros((16, 1), jnp.int32)
        for t in range(STEPS):
            var_col = jnp.where((rowh >> 2) == t, nvar[r, t], var_col)
        biases.append(jnp.where(cvar[r:r + 1, :] == var_col, same_col, other_col))

    arrived(xg.at[0:TP - 1], 0)
    for r in range(REQ):
        for j in range(TP):
            slab = xg[j, r].astype(F32)
            xf[STEPS * r:STEPS * r + STEPS, LW * j:LW * j + LW] = slab
            xb[2 * r, :, LW * j:LW * j + LW] = slab[0:2, :]
            xb[2 * r + 1, :, LW * j:LW * j + LW] = slab[2:4, :]

    def norm(values, gain_ref):
        square = jnp.sum(values * values, axis=1, keepdims=True)
        gain = gain_ref[...].astype(F32).reshape(1, D)
        return (values * lax.rsqrt(square / D + EPS) * gain).astype(BF16)

    normed = norm(xf[...], again)
    for copy in qkv_copies:
        copy.wait()
    lane2 = iota((TOK, LW), 1)

    def rope(values):
        swapped = jnp.where(
            (lane2 & 32) == 0, pltpu.roll(values, LW - 32, 1), pltpu.roll(values, 32, 1)
        )
        return (values * cosine + swapped * sine).astype(BF16)

    queries = rope(dot(normed, wq[...]))
    keys = rope(dot(normed, wk[...]))
    values = dot(normed, wv[...]).astype(BF16)

    pick = jnp.where((iota((64, TOK), 0) >> 2) == iota((64, TOK), 1), 1.0, 0.0).astype(BF16)
    spread = dot(pick, queries)
    head_lane = (iota((64, LW), 1) >> 6) == (iota((64, LW), 0) & 3)
    spread = jnp.where(head_lane, spread, 0.0).astype(BF16)

    def state(total, peak, sums, rows):
        mine = (iota((rows, LW), 1) >> 6) == (iota((rows, LW), 0) & 3)
        sums = jnp.where(mine, sums, 0.0)
        folded = sums[:, 0:128] + sums[:, 128:256]
        folded = folded + pltpu.roll(folded, 64, 1)
        at = iota((rows, 128), 1)
        return jnp.where(at < 64, folded, jnp.where(at < 96, total, peak))

    for r in range(REQ):
        k_copies[r].wait()
        scores = dot_t(spread[16 * r:16 * r + 16, :], ck[r]) * SCALE + biases[r]
        scores = jnp.where(usable[r] == 1, scores, NEG)
        peak = jnp.max(scores, axis=1, keepdims=True)
        raw = jnp.where(usable[r] == 1, jnp.exp(scores - peak), 0.0)
        total = jnp.sum(raw, axis=1, keepdims=True)
        v_copies[r].wait()
        sums = dot(raw.astype(BF16), cv[r])
        block = state(total, peak, sums, 16)
        sbuf[2 * r] = block[0:8, :]
        sbuf[2 * r + 1] = block[8:16, :]

    for d in range(1, NB):
        other, peer = b_peer(d)
        send(sbuf.at[other], rslots.at[b], 1, peer)

    keys32 = keys.astype(F32)
    values32 = values.astype(F32)
    for r in range(REQ):
        nk_v[r] = keys32[STEPS * r:STEPS * r + STEPS, :].astype(BF16)
        nv_v[r] = values32[STEPS * r:STEPS * r + STEPS, :].astype(BF16)
    nk_copy = pltpu.make_async_copy(nk_v, nk_out, osem.at[0])
    nv_copy = pltpu.make_async_copy(nv_v, nv_out, osem.at[1])
    nk_copy.start()
    nv_copy.start()
    row64 = iota((64, 1), 0)
    col16 = iota((1, TOK), 1)
    same64 = jnp.zeros((64, 1), F32)
    other64 = jnp.zeros((64, 1), F32)
    for h in range(LH):
        same64 = jnp.where((row64 & 3) == h, bias[0, i * LH + h], same64)
        other64 = jnp.where((row64 & 3) == h, bias[1, i * LH + h], other64)
    var64 = jnp.zeros((64, 1), jnp.int32)
    var16 = jnp.zeros((1, TOK), jnp.int32)
    for n in range(TOK):
        token_variate = nvar[n // STEPS, n % STEPS]
        var64 = jnp.where((row64 >> 2) == n, token_variate, var64)
        var16 = jnp.where(col16 == n, token_variate, var16)
    new_scores = dot_t(spread, keys) * SCALE + jnp.where(var64 == var16, same64, other64)
    row_token = row64 >> 2
    causal = ((col16 >> 2) == (row_token >> 2)) & ((col16 & 3) <= (row_token & 3))
    new_scores = jnp.where(causal, new_scores, NEG)
    new_peak = jnp.max(new_scores, axis=1, keepdims=True)
    new_raw = jnp.where(causal, jnp.exp(new_scores - new_peak), 0.0)
    new_total = jnp.sum(new_raw, axis=1, keepdims=True)
    new_sums = dot(new_raw.astype(BF16), values)
    new_state = state(new_total, new_peak, new_sums, 64)
    for k in range(NB):
        nbuf[k] = new_state[8 * k:8 * k + 8, :]
    rslots[b] = sbuf[b]

    arrived(rslots.at[0:NB - 1], 1)
    joined, peak = merge([rslots[k] for k in range(NB)])
    lane8 = iota((8, 128), 1)
    zslots[z] = jnp.where(lane8 < 96, joined, peak)
    for d in range(1, NZ):
        send(zslots.at[z], zslots.at[z], 2, z_peer(d))
    arrived(zslots.at[0:NZ - 1], 2)
    joined, _ = merge([zslots[k] for k in range(NZ)] + [nbuf[b]])
    attention = joined / joined[:, 64:65]
    attention = jnp.where(lane8 < 64, attention, pltpu.roll(attention, 64, 1))
    attention = jnp.concatenate([attention, attention], axis=1)
    row8 = iota((8, LW), 0)
    attention = jnp.where((iota((8, LW), 1) >> 6) == (row8 & 3), attention, 0.0)
    first = jnp.sum(jnp.where(row8 < 4, attention, 0.0), axis=0, keepdims=True)
    second = jnp.sum(jnp.where(row8 < 4, 0.0, attention), axis=0, keepdims=True)
    attention = jnp.where(row8 == 0, first, second).astype(BF16)

    wo_copy.wait()
    cslots[i] = dot(attention, wo[...])[0:2, :]
    for d in range(1, TP):
        send(cslots.at[i], cslots.at[i], 3, tp_peer(d))
    arrived(cslots.at[0:TP - 1], 3)
    middle = xb[b] + (cslots[0] + cslots[1] + cslots[2] + cslots[3])
    midall[b] = middle.astype(BF16)
    for d in range(1, NB):
        send(midall.at[b], midall.at[b], 4, b_peer(d)[1])
    arrived(midall.at[0:NB - 1], 4)
    for k in range(NB):
        midf[2 * k:2 * k + 2, :] = midall[k].astype(F32)

    middle = midf[...]
    for j in range(TP):
        midc[j] = middle[:, LW * j:LW * j + LW]
    normed_two = norm(middle, fgain)
    wg_copy.wait()
    gate = dot(normed_two, wg[...])
    wu_copy.wait()
    up = dot(normed_two, wu[...])
    activated = (gate / (1.0 + jnp.exp(-gate)) * up).astype(BF16)
    wd_copy.wait()
    down = dot(activated, wd[...])
    for j in range(TP):
        dbuf[j] = down[:, LW * j:LW * j + LW]
    for d in range(1, TP):
        send(dbuf.at[lax.rem(i + d, TP)], dslots.at[i], 5, tp_peer(d))
    dslots[i] = dbuf[i]
    arrived(dslots.at[0:TP - 1], 5)
    hidden = midc[i] + (dslots[0] + dslots[1] + dslots[2] + dslots[3])
    for r in range(REQ):
        hid_v[r] = hidden[STEPS * r:STEPS * r + STEPS, :].astype(BF16)
    hid_copy = pltpu.make_async_copy(hid_v, hid_out, osem.at[2])
    hid_copy.start()
    for copy in sends:
        copy.wait_send()
    nk_copy.wait()
    nv_copy.wait()
    hid_copy.wait()


def on_device(*args):
    inverse = np.exp(
        np.float32(-math.log(10000.0)) * (np.arange(32, dtype=np.float32) * np.float32(2.0 / 64))
    ).astype(np.float32)
    inverse = jnp.asarray(np.tile(inverse, 4)[None, :])
    vmem, smem = pltpu.VMEM, pltpu.SMEM
    out = jax.ShapeDtypeStruct((REQ, STEPS, LW), BF16)
    any_spec = pl.BlockSpec(memory_space=pl.ANY)
    return pl.pallas_call(
        kernel,
        out_shape=(out, out, out),
        in_specs=[any_spec] * 20,
        out_specs=(any_spec,) * 3,
        scratch_shapes=[
            vmem((TP, REQ, STEPS, LW), BF16),
            vmem((D,), BF16), vmem((D,), BF16),
            vmem((D, LW), BF16), vmem((D, LW), BF16), vmem((D, LW), BF16),
            vmem((LW, D), BF16),
            vmem((D, D), BF16), vmem((D, D), BF16), vmem((D, D), BF16),
            smem((2, 16), F32),
            vmem((REQ, SPAN, LW), BF16), vmem((REQ, SPAN, LW), BF16),
            vmem((REQ, SPAN), jnp.int32), vmem((REQ, SPAN), jnp.int32),
            smem((REQ,), jnp.int32), smem((REQ,), jnp.int32),
            smem((REQ, STEPS), jnp.int32), smem((REQ, STEPS), jnp.int32),
            vmem((1, 128), F32),
            vmem((TOK, D), F32),
            vmem((NB, 2, D), F32),
            vmem((NB, 8, 128), F32),
            vmem((NB, 8, 128), F32),
            vmem((NB, 8, 128), F32),
            vmem((NZ, 8, 128), F32),
            vmem((TP, 2, D), F32),
            vmem((NB, 2, D), BF16),
            vmem((TOK, D), F32),
            vmem((TP, TOK, LW), F32),
            vmem((TP, TOK, LW), F32),
            vmem((TP, TOK, LW), F32),
            vmem((REQ, STEPS, LW), BF16),
            vmem((REQ, STEPS, LW), BF16),
            vmem((REQ, STEPS, LW), BF16),
            pltpu.SemaphoreType.DMA((32,)),
            pltpu.SemaphoreType.DMA((3,)),
            pltpu.SemaphoreType.DMA((32,)),
            pltpu.SemaphoreType.DMA((6,)),
        ],
        compiler_params=pltpu.CompilerParams(
            collective_id=0, has_side_effects=True, vmem_limit_bytes=48 * 1024 * 1024
        ),
        name="layer",
    )(*args, inverse)


def solution(mesh):
    return jax.shard_map(
        on_device,
        mesh=mesh,
        in_specs=(
            P(None, None, "tp"),
            P(),
            P(),
            P(None, "tp"),
            P(None, "tp"),
            P(None, "tp"),
            P("tp", None),
            P(None, "tp"),
            P(None, "tp"),
            P("tp", None),
            P(),
            P(None, "seq", "tp"),
            P(None, "seq", "tp"),
            P(None, "seq"),
            P(None, "seq"),
            P(),
            P(),
            P(),
            P(),
        ),
        out_specs=(P(None, None, "tp"), P(None, None, "tp"), P(None, None, "tp")),
        check_vma=False,
    )
```
